32 devices in a mesh: grp: 2 (over x), ord: 16 (over z, y, core).
Axes of the slice: x: 2, y: 2, z: 4, core: 2. Of those that a mesh axis runs over, the one named last changes fastest.
Arguments:
- grid: bfloat16 [1024, 1024, 256], P(('grp', 'ord')), parts along dimension 0, may hold values from -6 to 6
- legendre: bfloat16 [16, 64, 512, 512], P('ord'), as said below
- mixing: bfloat16 [512, 2, 256, 256], P('ord'), may hold values from -0.25 to 0.25
Outputs:
- spectrum: bfloat16 [1024, 512, 512], P(('grp', 'ord')), parts along dimension 0
The draws below stay inside these ranges and needn't reach their ends.
There are 2 independent parts, one for each index of `grp`. The reference program is written for one: setup_inputs(seed, part) draws one part's arguments, and reference() takes and returns one part's arrays. A program takes and returns all parts, laid end to end along the dimension named above; an argument that names none is the same for every part. Nothing has to cross between parts.
Inputs may be any that keep to these rules, and one draw needn't show every extreme that they name: `legendre`: entries whose degree is below their order are zero. The slots 32 to 63 of block index b repeat the panels that block index 16 - 1 - b holds in its slots 0 to 31.
All inputs are finite; a program needn't handle non-finite values.
Results may differ from the reference program's by a relative error of at most 0.0062.
Values may be sent and summed in bfloat16 or wider, within the bound.
No kernel may reach another device: no remote copies, remote signals or barrier semaphores. Data moves between devices by JAX's collectives and lax.ppermute only.
A program may use at most 256 MiB of HBM per device.

```python
import math
import jax
import jax.numpy as jnp
from jax import lax

C = 256
M = 512
L = 512
NLAT = 512
NLON = 1024
OB = 32


def draw_legendre(key, part):
    scale = 1.0 / math.sqrt(NLAT)
    base = jax.random.normal(key, (M, L, NLAT), jnp.float32) * scale
    order = jnp.arange(M)[:, None, None]
    degree = jnp.arange(L)[None, :, None]
    base = jnp.where(degree >= order, base, 0.0)
    own = base.reshape(M // OB, OB, L, NLAT)
    return jnp.concatenate([own, own[::-1]], axis=1).astype(jnp.bfloat16)


def shard_levels(key, dims, cuts, low, high):
    loudness = 1.0
    for dim, parts in cuts:
        heights = jax.random.uniform(jax.random.fold_in(jax.random.fold_in(key, 6), dim), (parts,), jnp.float32, low / len(cuts), high / len(cuts))
        loudness = loudness * jnp.repeat(jnp.exp(heights), dims[dim] // parts).reshape((-1,) + (1,) * (len(dims) - 1 - dim))
    return loudness


def normal_values(own_key, dims, deviation, limit, cuts=(), held_as=jnp.bfloat16):
    entries = deviation * jax.random.normal(own_key, dims, jnp.float32)
    if cuts:
        entries = entries * shard_levels(own_key, dims, cuts, -0.22, 0.18)
    return jnp.clip(entries, -limit, limit).astype(held_as)


def setup_inputs(seed: int = 0, part: int = 0) -> dict:
    keys = jax.random.split(jax.random.key(seed), 4)
    part_keys = jax.random.split(jax.random.fold_in(keys[3], part), 4)
    return {
        "grid": normal_values(part_keys[0], (NLAT, NLON, C), 1.0, 6.0, ((0, 16),)),
        "legendre": draw_legendre(jax.random.fold_in(keys[3], 71), part),
        "mixing": normal_values(keys[2], (L, 2, C, C), (2 * C) ** -0.5, 0.25, ((0, 16),)),
    }


def fourier_table(nlon, orders):
    longitude = jnp.arange(nlon, dtype=jnp.int32)
    order = jnp.arange(orders, dtype=jnp.int32)
    phase = longitude[:, None] * order[None, :] % nlon
    angle = phase.astype(jnp.float32) * (2.0 * math.pi / nlon)
    scale = 1.0 / math.sqrt(nlon)
    table = jnp.stack([jnp.cos(angle) * scale, -jnp.sin(angle) * scale], axis=-1)
    return table.reshape(nlon, 2 * orders).astype(jnp.bfloat16)

def reference(grid, legendre, mixing):
    blocks = M // OB
    table = fourier_table(NLON, M)
    fourier = jnp.einsum('tnc,nk->tkc', grid.astype(jnp.float32), table.astype(jnp.float32))
    fourier = fourier.astype(jnp.bfloat16).reshape(NLAT, blocks, OB, 2 * C)
    fourier = jnp.transpose(fourier, (1, 0, 2, 3))
    panels = legendre[:, :OB]

    def analyse(pair):
        panel, spectra = pair
        result = jnp.einsum('mlt,tmk->mlk', panel.astype(jnp.float32), spectra.astype(jnp.float32))
        return result.astype(jnp.bfloat16)
    coeff = lax.map(analyse, (panels, fourier)).reshape(M, L, 2 * C)
    coeff = jnp.transpose(coeff, (1, 0, 2))
    real_part = mixing[:, 0]
    imag_part = mixing[:, 1]
    block_weight = jnp.concatenate([jnp.concatenate([real_part, imag_part], axis=-1), jnp.concatenate([-imag_part, real_part], axis=-1)], axis=1)

    def combine(pair):
        values, weight = pair
        return jnp.dot(values.astype(jnp.float32), weight.astype(jnp.float32)).astype(jnp.bfloat16)
    return lax.map(combine, (coeff, block_weight))
```

```python
import functools
import math

import jax
import jax.numpy as jnp
import ml_dtypes
import numpy as np
from jax import lax
from jax.experimental import pallas as pl
from jax.experimental.pallas import tpu as pltpu
from jax.sharding import PartitionSpec as P

CHUNK = 8
PARTS = 2
TILE = 16
VMEM_LIMIT = 56 << 20


def fourier_table(nlon, count, per_dev, first, size):
    owner = np.arange(count)[:, None]
    order = ((count - 1 - owner) * per_dev + first + np.arange(size)[None, :]).reshape(-1)
    phase = order[:, None] * np.arange(nlon)[None, :] % nlon
    angle = phase.astype(np.float32) * np.float32(2.0 * math.pi / nlon)
    scale = np.float32(1.0 / math.sqrt(nlon))
    table = np.concatenate([np.cos(angle) * scale, -np.sin(angle) * scale], axis=0)
    return table.astype(ml_dtypes.bfloat16)


def swap_matrix(outer, inner):
    rows = np.arange(outer * inner)
    source = rows % outer * inner + rows // outer
    return (source[:, None] == rows[None, :]).astype(ml_dtypes.bfloat16)


def fourier_kernel(rows_step, table_ref, swap_ref, grid_ref, out_ref, hold):
    group, rows, chans = hold.shape
    pairs = rows // 2
    steps = group // rows_step
    part = lax.rem(pl.program_id(0), steps)
    for row in range(rows_step):
        result = jnp.dot(table_ref[...], grid_ref[row], preferred_element_type=jnp.float32)
        hold[part * rows_step + row] = result.astype(jnp.bfloat16)

    @pl.when(part == steps - 1)
    def _():
        for first in range(0, rows, TILE):
            values = hold[:, first : first + TILE, :].reshape(group * TILE, chans)
            swapped = jnp.dot(swap_ref[...], values, preferred_element_type=jnp.float32)
            p, pair = first // pairs, first % pairs
            out_ref[pair : pair + TILE, :, p * chans : (p + 1) * chans] = swapped.astype(jnp.bfloat16).reshape(
                TILE, group, chans
            )


def fourier(grid, table, count, size):
    lat_rows, nlon, chans = grid.shape
    pairs = count * size
    if lat_rows % TILE or pairs % TILE:
        result = jnp.einsum("rn,tnc->rtc", table, grid, preferred_element_type=jnp.float32).astype(jnp.bfloat16)
        result = result.reshape(2, count, size, lat_rows, chans).transpose(1, 2, 3, 0, 4)
        return result.reshape(count, size, lat_rows, 2 * chans)
    rows_step = 4
    out = pl.pallas_call(
        functools.partial(fourier_kernel, rows_step),
        out_shape=jax.ShapeDtypeStruct((pairs, lat_rows, 2 * chans), jnp.bfloat16),
        grid=(lat_rows // rows_step,),
        in_specs=[
            pl.BlockSpec(table.shape, lambda g: (0, 0)),
            pl.BlockSpec((TILE * TILE, TILE * TILE), lambda g: (0, 0)),
            pl.BlockSpec((rows_step, nlon, chans), lambda g: (g, 0, 0)),
        ],
        out_specs=pl.BlockSpec((pairs, TILE, 2 * chans), lambda g: (0, g // (TILE // rows_step), 0)),
        scratch_shapes=[pltpu.VMEM((TILE, 2 * pairs, chans), jnp.bfloat16)],
        compiler_params=pltpu.CompilerParams(vmem_limit_bytes=VMEM_LIMIT),
        cost_estimate=pl.CostEstimate(
            flops=4 * pairs * nlon * chans * lat_rows,
            bytes_accessed=2 * (grid.size + table.size + pairs * lat_rows * 2 * chans),
            transcendentals=0,
        ),
        name="fourier",
    )(table, jnp.asarray(swap_matrix(TILE, TILE)), grid)
    return out.reshape(count, size, lat_rows, 2 * chans)


def legendre_kernel(tile, parts, block_ref, panel_ref, swap_ref, *rest):
    spectra_refs, far_refs, hold = rest[:parts], rest[parts:-1], rest[-1]
    degrees, latitudes = panel_ref.shape[2:]
    span, size, width = far_refs[0].shape
    block = block_ref[0]
    j = pl.program_id(0)

    def advance(spectra_ref):
        values = spectra_ref[:, 0].reshape(latitudes, width)
        for t in range(degrees // tile):

            @pl.when((t + 1) * tile > block * span)
            def _():
                part = jnp.dot(
                    panel_ref[0, 0, t * tile : (t + 1) * tile, :], values, preferred_element_type=jnp.float32
                )
                hold[j, t * tile : (t + 1) * tile, :] = part.astype(jnp.bfloat16)

    for index, spectra_ref in enumerate(spectra_refs):
        pl.when(j // (size // parts) == index)(functools.partial(advance, spectra_ref))

    @pl.when(j == size - 1)
    def _():
        for k in range(len(far_refs)):
            degree = jnp.bitwise_xor(block, k)

            @pl.when(degree >= block)
            def _():
                for first in range(0, span, TILE):
                    start = pl.multiple_of(degree * span + first, TILE)
                    values = hold[:, pl.ds(start, TILE), :].reshape(size * TILE, width)
                    swapped = jnp.dot(swap_ref[...], values, preferred_element_type=jnp.float32)
                    far_refs[k][first : first + TILE] = swapped.astype(jnp.bfloat16).reshape(TILE, size, width)


def legendre_part(block, legendre, spectra, first):
    count, part_size, lat_rows, width = spectra[0].shape
    parts = len(spectra)
    size = parts * part_size
    _, panels, degrees, latitudes = legendre.shape
    span = degrees // count
    base = panels // 2 + first
    if size % TILE or span % TILE or lat_rows % TILE:
        values = jnp.concatenate(spectra, axis=1).transpose(0, 2, 1, 3).reshape(latitudes, size, width)
        panel = legendre[0, base : base + size]
        result = jnp.einsum("jlt,tjk->ljk", panel, values, preferred_element_type=jnp.float32)
        result = result.astype(jnp.bfloat16).reshape(count, span, size, width)
        return [lax.dynamic_index_in_dim(result, block[0] ^ k, keepdims=False) for k in range(count)]
    tile = min(128, degrees)
    piece = jax.ShapeDtypeStruct((span, size, width), jnp.bfloat16)

    def spectra_spec(part):
        def where(j, b):
            return 0, jnp.clip(j - part * part_size, 0, part_size - 1), 0, 0

        return pl.BlockSpec((count, 1, lat_rows, width), where)

    return pl.pallas_call(
        functools.partial(legendre_kernel, tile, parts),
        out_shape=[piece] * count,
        grid_spec=pltpu.PrefetchScalarGridSpec(
            num_scalar_prefetch=1,
            grid=(size,),
            in_specs=[
                pl.BlockSpec((1, 1, degrees, latitudes), lambda j, b: (0, base + j, 0, 0)),
                pl.BlockSpec((size * TILE, size * TILE), lambda j, b: (0, 0)),
            ]
            + [spectra_spec(part) for part in range(parts)],
            out_specs=[pl.BlockSpec((span, size, width), lambda j, b: (0, 0, 0))] * count,
            scratch_shapes=[pltpu.VMEM((size, degrees, width), jnp.bfloat16)],
        ),
        compiler_params=pltpu.CompilerParams(vmem_limit_bytes=VMEM_LIMIT),
        cost_estimate=pl.CostEstimate(
            flops=2 * size * degrees * latitudes * width,
            bytes_accessed=2 * size * (degrees * latitudes + 2 * degrees * width),
            transcendentals=0,
        ),
        name="legendre",
    )(block, legendre, jnp.asarray(swap_matrix(size, TILE)), *spectra)


def mixing_kernel(index_ref, mixing_ref, *rest):
    out_ref, hold = rest[-2:]
    _, count, size, width = out_ref.shape
    far_refs = rest[:count]
    chans = width // 2
    me = index_ref[0]
    for row in range(out_ref.shape[0]):
        for k in range(count):
            hold[jnp.bitwise_xor(me, k)] = far_refs[k][row]
        values = hold[...].reshape(count * size, width)
        real, imag = values[:, :chans], values[:, chans:]
        real_w, imag_w = mixing_ref[row, 0], mixing_ref[row, 1]
        out_real = jnp.dot(real, real_w, preferred_element_type=jnp.float32) - jnp.dot(
            imag, imag_w, preferred_element_type=jnp.float32
        )
        out_imag = jnp.dot(real, imag_w, preferred_element_type=jnp.float32) + jnp.dot(
            imag, real_w, preferred_element_type=jnp.float32
        )
        out_ref[row, :, :, :chans] = out_real.astype(jnp.bfloat16).reshape(count, size, chans)
        out_ref[row, :, :, chans:] = out_imag.astype(jnp.bfloat16).reshape(count, size, chans)


def mix_part(index, mixing, far, before, chunk, per_dev):
    count = len(far)
    span, size, width = far[0].shape
    chans = width // 2
    if size % TILE:
        stack = jnp.stack([far[k] for k in range(count)])
        stack = jnp.take(stack, jnp.arange(count) ^ index[0], axis=0)
        real_w, imag_w = mixing[:, 0], mixing[:, 1]
        weight = jnp.concatenate(
            [jnp.concatenate([real_w, imag_w], axis=-1), jnp.concatenate([-imag_w, real_w], axis=-1)], axis=1
        )
        mixed = jnp.einsum("bljk,lkn->lbjn", stack, weight, preferred_element_type=jnp.float32)
        return mixed.astype(jnp.bfloat16)
    step = min(2, span)
    operands = [index, mixing, *far]
    specs = [
        pl.BlockSpec((step, 2, chans, chans), lambda l, i: (l, 0, 0, 0)),
    ] + [pl.BlockSpec((step, size, width), lambda l, i: (l, 0, 0))] * count
    aliases = {}
    if before is not None:
        aliases = {len(operands): 0}
        operands.append(before)
        specs.append(pl.BlockSpec(memory_space=pl.ANY))
    return pl.pallas_call(
        mixing_kernel,
        out_shape=jax.ShapeDtypeStruct((span, count, per_dev, width), jnp.bfloat16),
        grid_spec=pltpu.PrefetchScalarGridSpec(
            num_scalar_prefetch=1,
            grid=(span // step,),
            in_specs=specs,
            out_specs=pl.BlockSpec((step, count, size, width), lambda l, i: (l, 0, chunk, 0)),
            scratch_shapes=[pltpu.VMEM((count, size, width), jnp.bfloat16)],
        ),
        input_output_aliases=aliases,
        compiler_params=pltpu.CompilerParams(vmem_limit_bytes=VMEM_LIMIT),
        cost_estimate=pl.CostEstimate(
            flops=2 * span * count * size * width * width,
            bytes_accessed=2 * (mixing.size + 2 * span * count * size * width),
            transcendentals=0,
        ),
        name="mix",
    )(*operands)


def on_device(grid, legendre, mixing):
    count = lax.axis_size("ord")
    half = count // 2
    me = lax.axis_index("ord")
    index = me.astype(jnp.int32).reshape(1)
    block = count - 1 - index
    nlon = grid.shape[1]
    per_dev = legendre.shape[1] // 2
    size = min(CHUNK, per_dev)
    chunks = per_dev // size
    parts = min(PARTS, chunks)
    stages = chunks // parts
    rounds = [r for k in range(half) for r in (k, half + k)]
    tables = [jnp.asarray(fourier_table(nlon, count, per_dev, q * size, size)) for q in range(chunks)]
    sending = [fourier(grid, table, count, size) for table in tables]

    def exchange(values):
        return lax.all_to_all(values, "ord", split_axis=0, concat_axis=0, tiled=True)

    def deliver(far):
        landed = [None] * count
        for k in rounds:
            pairs = [(count - 1 - b, b ^ k) for b in range(count) if b ^ k >= b]
            landed[k] = lax.ppermute(far[k], "ord", pairs)
        return landed

    arrived = [exchange(values) for values in sending]
    out = None
    for stage in range(stages):
        first = stage * parts
        far = legendre_part(block, legendre, arrived[first : first + parts], first * size)
        landed = deliver(far)
        out = mix_part(index, mixing, landed, out, stage, per_dev)
    span, _, _, width = out.shape
    return out.reshape(span, count * per_dev, width)


def solution(mesh):
    return jax.shard_map(
        on_device,
        mesh=mesh,
        in_specs=(
            P(("grp", "ord"), None, None),
            P("ord", None, None, None),
            P("ord", None, None, None),
        ),
        out_specs=P(("grp", "ord"), None, None),
        check_vma=False,
    )
```

```python
import functools
import math

import jax
import jax.numpy as jnp
import ml_dtypes
import numpy as np
from jax import lax
from jax.experimental import pallas as pl
from jax.experimental.pallas import tpu as pltpu
from jax.sharding import PartitionSpec as P

STAGES = 2
WINDOW = 5
TILE = 16
VMEM_LIMIT = 56 << 20


def fourier_table(nlon, count, per_dev, first, size):
    owner = np.arange(count)[:, None]
    order = (count - 1 - owner) * per_dev + first + np.arange(size)[None, :]
    phase = order[:, :, None] * np.arange(nlon) % nlon
    angle = phase.astype(np.float32) * np.float32(2.0 * math.pi / nlon)
    scale = np.float32(1.0 / math.sqrt(nlon))
    table = np.stack([np.cos(angle) * scale, -np.sin(angle) * scale], axis=1)
    return table.astype(ml_dtypes.bfloat16)


def swap_matrix(outer, inner):
    rows = np.arange(outer * inner)
    source = rows % outer * inner + rows // outer
    return (source[:, None] == rows[None, :]).astype(ml_dtypes.bfloat16)


def fourier_kernel(rows_step, index_ref, table_ref, swap_ref, grid_ref, *rest):
    out_refs, hold = rest[:-1], rest[-1]
    half, _, size, nlon = table_ref.shape
    group, rows, chans = hold.shape
    steps = group // rows_step
    part = lax.rem(pl.program_id(0), steps)
    table = table_ref[...].reshape(rows, nlon)
    for row in range(rows_step):
        result = jnp.dot(table, grid_ref[row], preferred_element_type=jnp.float32)
        hold[part * rows_step + row] = result.astype(jnp.bfloat16)

    @pl.when(part == steps - 1)
    def _():
        for k in range(half):
            owner = jnp.bitwise_xor(lax.rem(index_ref[0], half), k)
            for p in range(2):
                for first in range(0, size, TILE):
                    start = pl.multiple_of((owner * 2 + p) * size + first, TILE)
                    values = hold[:, pl.ds(start, TILE), :].reshape(group * TILE, chans)
                    swapped = jnp.dot(swap_ref[...], values, preferred_element_type=jnp.float32)
                    out_refs[k][first : first + TILE, :, p * chans : (p + 1) * chans] = swapped.astype(
                        jnp.bfloat16
                    ).reshape(TILE, group, chans)


def fourier(index, grid, table, crossing):
    lat_rows, nlon, chans = grid.shape
    count, _, size, _ = table.shape
    half = count // 2
    table = jnp.asarray(table)
    if lat_rows % TILE or size % TILE:
        result = jnp.einsum("ipjn,tnc->ijtpc", table, grid, preferred_element_type=jnp.float32)
        result = result.astype(jnp.bfloat16).reshape(count, size, lat_rows, 2 * chans)
        base = half if crossing else 0
        return [lax.dynamic_index_in_dim(result, index[0] ^ (base + k), keepdims=False) for k in range(half)]
    rows_step = 4
    steps = TILE // rows_step

    def side(g, i):
        mine = i[0] // half
        return (1 - mine if crossing else mine), 0, 0, 0

    rows = 2 * half * size
    return pl.pallas_call(
        functools.partial(fourier_kernel, rows_step),
        out_shape=[jax.ShapeDtypeStruct((size, lat_rows, 2 * chans), jnp.bfloat16)] * half,
        grid_spec=pltpu.PrefetchScalarGridSpec(
            num_scalar_prefetch=1,
            grid=(lat_rows // rows_step,),
            in_specs=[
                pl.BlockSpec((half, 2, size, nlon), side),
                pl.BlockSpec((TILE * TILE, TILE * TILE), lambda g, i: (0, 0)),
                pl.BlockSpec((rows_step, nlon, chans), lambda g, i: (g, 0, 0)),
            ],
            out_specs=[pl.BlockSpec((size, TILE, 2 * chans), lambda g, i: (0, g // steps, 0))] * half,
            scratch_shapes=[pltpu.VMEM((TILE, rows, chans), jnp.bfloat16)],
        ),
        compiler_params=pltpu.CompilerParams(vmem_limit_bytes=VMEM_LIMIT),
        cost_estimate=pl.CostEstimate(
            flops=2 * rows * nlon * chans * lat_rows,
            bytes_accessed=2 * (grid.size + rows * nlon + rows * lat_rows * chans),
            transcendentals=0,
        ),
        name="fourier",
    )(index, table, jnp.asarray(swap_matrix(TILE, TILE)), grid)


def legendre_kernel(skip, index_ref, panel_ref, swap_ref, *rest):
    count = len(rest) // 2 - 1
    spectra_refs, far_refs, values, hold = rest[:count], rest[count:-2], rest[-2], rest[-1]
    degrees, latitudes = panel_ref.shape[2:]
    span, size, width = far_refs[-1].shape
    me = index_ref[0]
    block = count - 1 - me
    j = pl.program_id(0)
    for k in range(count):
        values[jnp.bitwise_xor(me, k)] = spectra_refs[k][0]
    spectra = values[...].reshape(latitudes, width)

    def advance(first):
        part = jnp.dot(panel_ref[0, 0, first:, :], spectra, preferred_element_type=jnp.float32)
        hold[j, first:, :] = part.astype(jnp.bfloat16)

    pl.when(block < count // 2)(functools.partial(advance, 0))
    pl.when(block >= count // 2)(functools.partial(advance, degrees // 2))

    @pl.when(j == size - 1)
    def _():
        for k in range(count):
            degree = jnp.bitwise_xor(block, k)

            @pl.when(degree >= block)
            def _():
                lost = skip if k == 0 else 0
                for first in range(lost, span, TILE):
                    start = pl.multiple_of(degree * span + first, TILE)
                    pieces = hold[:, pl.ds(start, TILE), :].reshape(size * TILE, width)
                    swapped = jnp.dot(swap_ref[...], pieces, preferred_element_type=jnp.float32)
                    far_refs[k][first - lost : first - lost + TILE] = swapped.astype(jnp.bfloat16).reshape(TILE, size, width)


def legendre_part(index, legendre, spectra, first):
    count = len(spectra)
    size, lat_rows, width = spectra[0].shape
    _, panels, degrees, latitudes = legendre.shape
    span = degrees // count
    base = panels // 2 + first
    if size % TILE or span % TILE or lat_rows % TILE:
        values = jnp.take(jnp.stack(spectra), jnp.arange(count) ^ index[0], axis=0)
        values = values.transpose(0, 2, 1, 3).reshape(latitudes, size, width)
        panel = legendre[0, base : base + size]
        result = jnp.einsum("jlt,tjk->ljk", panel, values, preferred_element_type=jnp.float32)
        result = result.astype(jnp.bfloat16).reshape(count, span, size, width)
        block = count - 1 - index[0]
        return [lax.dynamic_index_in_dim(result, block ^ k, keepdims=False) for k in range(count)]
    skip = min(first, span - TILE) // TILE * TILE
    spans = [span - skip] + [span] * (count - 1)
    return pl.pallas_call(
        functools.partial(legendre_kernel, skip),
        out_shape=[jax.ShapeDtypeStruct((rows, size, width), jnp.bfloat16) for rows in spans],
        grid_spec=pltpu.PrefetchScalarGridSpec(
            num_scalar_prefetch=1,
            grid=(size,),
            in_specs=[
                pl.BlockSpec((1, 1, degrees, latitudes), lambda j, i: (0, base + j, 0, 0)),
                pl.BlockSpec((size * TILE, size * TILE), lambda j, i: (0, 0)),
            ]
            + [pl.BlockSpec((1, lat_rows, width), lambda j, i: (j, 0, 0))] * count,
            out_specs=[pl.BlockSpec((rows, size, width), lambda j, i: (0, 0, 0)) for rows in spans],
            scratch_shapes=[
                pltpu.VMEM((count, lat_rows, width), jnp.bfloat16),
                pltpu.VMEM((size, degrees, width), jnp.bfloat16),
            ],
        ),
        compiler_params=pltpu.CompilerParams(vmem_limit_bytes=VMEM_LIMIT),
        cost_estimate=pl.CostEstimate(
            flops=2 * size * degrees * latitudes * width,
            bytes_accessed=2 * size * (degrees * latitudes + 2 * degrees * width),
            transcendentals=0,
        ),
        name="legendre",
    )(index, legendre, jnp.asarray(swap_matrix(size, TILE)), *spectra)


def mixing_kernel(first, count, skips, index_ref, mixing_ref, *rest):
    out_ref, hold = rest[-2:]
    rows, group, size, width = out_ref.shape
    piece_refs = rest[:group]
    chans = width // 2
    me = index_ref[0]
    inside = lax.rem(me, group)

    def advance(row, carry):
        degree = pl.program_id(0) * rows + row
        for n, skip in enumerate(skips):
            where = jnp.bitwise_xor(inside, n)
            piece = piece_refs[n][row]
            if first + n == count - 1:
                piece = jnp.where(jnp.bitwise_xor(me, count - 1) <= me, piece, jnp.zeros_like(piece))
            elif skip:
                piece = jnp.where(degree >= skip, piece, jnp.zeros_like(piece))
            hold[row, 0, where] = piece[:, :chans]
            hold[row, 1, where] = piece[:, chans:]
        values = hold[row].reshape(2 * group * size, chans)
        by_real = jnp.dot(values, mixing_ref[row, 0], preferred_element_type=jnp.float32)
        by_imag = jnp.dot(values, mixing_ref[row, 1], preferred_element_type=jnp.float32)
        half = group * size
        out_real = by_real[:half] - by_imag[half:]
        out_imag = by_imag[:half] + by_real[half:]
        out_ref[row, :, :, :chans] = out_real.astype(jnp.bfloat16).reshape(group, size, chans)
        out_ref[row, :, :, chans:] = out_imag.astype(jnp.bfloat16).reshape(group, size, chans)
        return carry

    lax.fori_loop(0, rows, advance, 0)


def mix_part(index, mixing, pieces, first, count, before, stage, per_dev):
    group = len(pieces)
    span, _, chans, _ = mixing.shape
    size, width = pieces[0].shape[1:]
    skips = [span - piece.shape[0] for piece in pieces]
    step = min(8, span)

    def piece_spec(skip):
        return pl.BlockSpec((step, size, width), lambda l, i: (jnp.maximum(l - skip // step, 0), 0, 0))

    operands = [index, mixing, *pieces]
    specs = [pl.BlockSpec((step, 2, chans, chans), lambda l, i: (l, 0, 0, 0))]
    specs += [piece_spec(skip) for skip in skips]
    aliases = {}
    if before is not None:
        aliases = {len(operands): 0}
        operands.append(before)
        specs.append(pl.BlockSpec(memory_space=pl.ANY))

    def where(l, i):
        return l, jnp.bitwise_xor(i[0], first) // group, stage, 0

    return pl.pallas_call(
        functools.partial(mixing_kernel, first, count, skips),
        out_shape=jax.ShapeDtypeStruct((span, count, per_dev, width), jnp.bfloat16),
        grid_spec=pltpu.PrefetchScalarGridSpec(
            num_scalar_prefetch=1,
            grid=(span // step,),
            in_specs=specs,
            out_specs=pl.BlockSpec((step, group, size, width), where),
            scratch_shapes=[pltpu.VMEM((step, 2, group, size, chans), jnp.bfloat16)],
        ),
        input_output_aliases=aliases,
        compiler_params=pltpu.CompilerParams(vmem_limit_bytes=VMEM_LIMIT),
        cost_estimate=pl.CostEstimate(
            flops=2 * span * group * size * width * width,
            bytes_accessed=2 * (mixing.size + 2 * span * group * size * width),
            transcendentals=0,
        ),
        name="mix",
    )(*operands)


def mix_plain(index, mixing, pieces):
    count = len(pieces)
    stack = jnp.take(jnp.stack(pieces), jnp.arange(count) ^ index[0], axis=0)
    held = jnp.arange(count) <= index[0]
    stack = jnp.where(held[:, None, None, None], stack, jnp.zeros_like(stack))
    real_w, imag_w = mixing[:, 0], mixing[:, 1]
    weight = jnp.concatenate(
        [jnp.concatenate([real_w, imag_w], axis=-1), jnp.concatenate([-imag_w, real_w], axis=-1)], axis=1
    )
    mixed = jnp.einsum("bljk,lkn->lbjn", stack, weight, preferred_element_type=jnp.float32)
    return mixed.astype(jnp.bfloat16)


def weave(stages, half):
    count = 2 * half
    main = [("a", s, k) for s in range(stages) for k in range(half, count)]
    main += [("c", s, k) for s in range(stages) for k in range(half)]
    beside = [[] for _ in main]
    for s in range(stages):
        for n, k in enumerate(range(half - 1, 0, -1)):
            where = s * half + 3 * half // 8 + n if s == 0 else s * half + half // 4 + n
            beside[min(where, len(main) - 1)].append(("a", s, k))
        for n, k in enumerate(range(half, count - 1)):
            where = half + half // 4 + n + s * (half + half // 8)
            beside[min(where, len(main) - 1)].append(("c", s, k))
    order = []
    for first, others in zip(main, beside):
        order.append(first)
        order += others
    return order


def on_device(grid, legendre, mixing):
    count = lax.axis_size("ord")
    half = count // 2
    index = lax.axis_index("ord").astype(jnp.int32).reshape(1)
    nlon = grid.shape[1]
    per_dev = legendre.shape[1] // 2
    stages = STAGES if per_dev % (STAGES * TILE) == 0 else 1
    size = per_dev // stages
    tables = [fourier_table(nlon, count, per_dev, s * size, size) for s in range(stages)]
    sends = {}
    landed = {}
    recent = []

    def after(value, key):
        value, landed[key] = lax.optimization_barrier((value, landed[key]))
        return value

    def spectra_to_send(stage, k):
        crossing = k >= half
        if (stage, crossing) not in sends:
            token = after(index, recent[-WINDOW]) if len(recent) >= WINDOW else index
            sends[stage, crossing] = fourier(token, grid, tables[stage], crossing)
        return sends[stage, crossing][k % half]

    coeffs = {}

    def coeffs_to_send(stage, k):
        if stage not in coeffs:
            for other in range(count):
                if ("a", stage, other) not in landed:
                    permute("a", stage, other)
            spectra = [landed["a", stage, other] for other in range(count)]
            coeffs[stage] = list(legendre_part(index, legendre, spectra, stage * size))
        return coeffs[stage][k]

    def permute(kind, stage, k):
        key = (kind, stage, k)
        if key in landed:
            return
        value = spectra_to_send(stage, k) if kind == "a" else coeffs_to_send(stage, k)
        if (kind == "a" and k == 0) or (kind == "c" and k == count - 1):
            landed[key] = value
            return
        if len(recent) >= WINDOW:
            value = after(value, recent[-WINDOW])
        if kind == "a":
            pairs = [(i, i ^ k) for i in range(count)]
        else:
            pairs = [(count - 1 - b, b ^ k) for b in range(count) if b ^ k >= b]
        landed[key] = lax.ppermute(value, "ord", pairs)
        recent.append(key)

    out = None
    mixed = [0] * stages
    done = []
    whole, split = [(0, count)], [(half, half), (0, half)]
    groups = [whole] * (stages - 1) + [split]

    def mix_ready(limit):
        nonlocal out
        for stage in range(stages):
            while stages > 1 and mixed[stage] < len(groups[stage]):
                first, group = groups[stage][mixed[stage]]
                keys = [("c", stage, k) for k in range(first, first + group)]
                if any(key in recent[limit:] or key not in landed for key in keys if key[2] != count - 1):
                    return
                mixed[stage] += 1
                if ("c", stage, count - 1) in keys:
                    permute("c", stage, count - 1)
                pieces = [landed[key] for key in keys]
                out = mix_part(index, mixing, pieces, first, count, out, stage, per_dev)
                done.append(len(recent))

    for kind, stage, k in weave(stages, half):
        mix_ready(max(len(recent) - WINDOW, 0))
        if done and kind == "c" and done[-1] == len(recent) and k < half:
            coeffs_to_send(stage, k)
            coeffs[stage][k], out = lax.optimization_barrier((coeffs[stage][k], out))
        permute(kind, stage, k)
    mix_ready(len(recent))
    if stages == 1:
        permute("c", 0, count - 1)
        out = mix_plain(index, mixing, [landed["c", 0, k] for k in range(count)])
    span, _, _, width = out.shape
    return out.reshape(span, count * per_dev, width)


def solution(mesh):
    return jax.shard_map(
        on_device,
        mesh=mesh,
        in_specs=(
            P(("grp", "ord"), None, None),
            P("ord", None, None, None),
            P("ord", None, None, None),
        ),
        out_specs=P(("grp", "ord"), None, None),
        check_vma=False,
    )
```
